32 devices in a mesh: seq: 16 (over z, y, core), chan: 2 (over x).
Axes of the slice: x: 2, y: 2, z: 4, core: 2. Of those that a mesh axis runs over, the one named last changes fastest.
Arguments:
- stream_in: bfloat16 [4096, 4096], P('seq'), may hold values from -6 to 6
- mr_proj: bfloat16 [4096, 3, 4096], P('seq', None, 'chan'), may hold values from -6 to 6
- mr_short: float32 [3, 3, 4096], P(None, None, 'chan'), may hold values from -3 to 3
- mr_filter: float32 [256, 128], P('chan'), may hold values from -0.5 to 0.5
- mr_out: bfloat16 [4096, 4096], P('chan', 'seq'), may hold values from -0.09375 to 0.09375
- li_gain: float32 [4096], replicated, may hold values from 0.5 to 1.5
- li_in: bfloat16 [4096, 3, 4096], P('seq', None, 'chan'), may hold values from -0.09375 to 0.09375
- li_short: float32 [3, 3, 4096], P(None, None, 'chan'), may hold values from -3 to 3
- li_res: float32 [16, 4096], P(None, 'chan'), may hold values from -0.09 to 0.09
- li_rate: float32 [16, 4096], P(None, 'chan'), may hold values from 0.00012207031 to 0.05
- li_skip: float32 [4096], P('chan'), may hold values from -4 to 4
Outputs:
- stream_out: bfloat16 [4096, 4096], P('seq', 'chan')
- li_output: bfloat16 [4096, 4096], P('chan', 'seq')
The draws below stay inside these ranges and needn't reach their ends.
All inputs are finite; a program needn't handle non-finite values.
Results may differ from the reference program's by a relative error of at most 0.04.
Values may be sent and summed in bfloat16 or wider, within the bound.
A program may use at most 128 MiB of HBM per device.

```python
import math
import jax
import jax.numpy as jnp
from jax import lax

D = 4096
KMR = 128
GROUP = 16
MODES = 16
SEQ_LEN = 4096
GROUPS = 256


def block_scale(own_key, dims, split, low, high):
    level, own = 1.0, jax.random.fold_in(own_key, 6)
    for axis_at, parts in split:
        draws = jnp.exp(jax.random.uniform(jax.random.fold_in(own, axis_at), (parts,), jnp.float32, low / len(split), high / len(split)))
        level = level * jnp.repeat(draws, dims[axis_at] // parts).reshape([-1 if axis == axis_at else 1 for axis in range(len(dims))])
    return level


def centred(key, shape, spread, limit, shards=(), kind=jnp.bfloat16):
    result = jax.random.normal(key, shape, jnp.float32) * spread
    if len(shards) > 0:
        result = block_scale(key, shape, shards, -0.22, 0.18) * result
    return jnp.clip(result, min=-limit, max=limit).astype(kind)


def setup_inputs(seed: int = 0) -> dict:
    key_list = jax.random.split(jax.random.key(seed), 12)
    stream_in = centred(key_list[0], (SEQ_LEN, D), 1.0, 6.0, ((0, 16),))
    mr_proj = centred(key_list[1], (SEQ_LEN, 3, D), 1.0, 6.0, ((0, 16), (2, 2)))
    mr_short = centred(key_list[2], (3, 3, D), 0.6, 3.0, ((2, 2),), jnp.float32)
    mr_filter = centred(key_list[3], (GROUPS, KMR), KMR ** -0.5, 0.5, ((0, 2),), jnp.float32)
    mr_out = centred(key_list[4], (D, D), D ** -0.5, 0.09375, ((0, 2), (1, 16)))
    li_gain = jnp.clip(1.0 + 0.1 * jax.random.normal(key_list[5], (D,), jnp.float32), 0.5, 1.5)
    li_in = centred(key_list[6], (D, 3, D), D ** -0.5, 0.09375, ((0, 16), (2, 2)))
    li_short = centred(key_list[7], (3, 3, D), 0.6, 3.0, ((2, 2),), jnp.float32)
    li_res = centred(key_list[8], (MODES, D), 0.015, 0.09, ((1, 2),), jnp.float32)
    li_rate = jnp.clip(jnp.exp(math.log(0.05) - 6.015181 * jax.random.uniform(key_list[9], (MODES, D), jnp.float32) ** block_scale(key_list[9], (MODES, D), ((1, 2),), -0.2, 0.2)), 0.00012207031, 0.05)
    li_skip = centred(key_list[10], (D,), 1.0, 4.0, ((0, 2),), jnp.float32)
    return dict(stream_in=stream_in, mr_proj=mr_proj, mr_short=mr_short, mr_filter=mr_filter, mr_out=mr_out, li_gain=li_gain, li_in=li_in, li_short=li_short, li_res=li_res, li_rate=li_rate, li_skip=li_skip)


EPSILON = 1e-06
HIGHEST = lax.Precision.HIGHEST

def short_filter(raw_rows, weights):
    row_count = raw_rows.shape[0]
    padded = jnp.concatenate([jnp.zeros((2,) + raw_rows.shape[1:], raw_rows.dtype), raw_rows], axis=0)
    running = weights[:, 0][None] * padded[2:2 + row_count]
    for lag_index in (1, 2):
        running = running + weights[:, lag_index][None] * padded[2 - lag_index:2 - lag_index + row_count]
    return running

def grouped_filter(values, filters):
    per_channel = jnp.repeat(filters, GROUP, axis=0)
    row_count = values.shape[0]
    tap_count = filters.shape[1]
    padded = jnp.concatenate([jnp.zeros((tap_count - 1, values.shape[1]), values.dtype), values], axis=0)

    def one_tap(lag_index, running):
        window = lax.dynamic_slice_in_dim(padded, tap_count - 1 - lag_index, row_count, 0)
        column = lax.dynamic_index_in_dim(per_channel, lag_index, 1, keepdims=False)
        return running + column[None] * window
    return lax.fori_loop(0, tap_count, one_tap, jnp.zeros_like(values))

def modal_long_filter(values, residues, rates, skip_gain):
    seq_length, chan_count = values.shape
    block_width = min(128, chan_count)
    block_count = chan_count // block_width
    lag_steps = jnp.arange(seq_length, dtype=jnp.float32)
    fft_length = 2 * seq_length

    def one_block(pieces_in):
        section, residue_set, rate_set, gain_set = pieces_in
        kernel = jnp.einsum('br,brl->bl', residue_set, jnp.exp(-rate_set[:, :, None] * lag_steps), precision=HIGHEST)
        spectrum = jnp.fft.rfft(section, n=fft_length) * jnp.fft.rfft(kernel, n=fft_length)
        convolved = jnp.fft.irfft(spectrum, n=fft_length)[:, :seq_length]
        return convolved + gain_set[:, None] * section
    channel_major = values.T.reshape(block_count, block_width, seq_length)
    residue_blocks = residues.T.reshape(block_count, block_width, residues.shape[0])
    rate_blocks = rates.T.reshape(block_count, block_width, rates.shape[0])
    gain_blocks = skip_gain.reshape(block_count, block_width)
    outputs = lax.map(one_block, (channel_major, residue_blocks, rate_blocks, gain_blocks))
    return outputs.reshape(chan_count, seq_length)

def reference(stream_in, mr_proj, mr_short, mr_filter, mr_out, li_gain, li_in, li_short, li_res, li_rate, li_skip):
    mr_mixed = short_filter(mr_proj.astype(jnp.float32), mr_short.astype(jnp.float32))
    mr_values = mr_mixed[:, 1] * mr_mixed[:, 2]
    mr_filtered = grouped_filter(mr_values, mr_filter.astype(jnp.float32))
    mr_gated = (mr_mixed[:, 0] * mr_filtered).astype(jnp.bfloat16)
    branch = jnp.dot(mr_gated, mr_out, preferred_element_type=jnp.float32)
    stream_out = (stream_in.astype(jnp.float32) + branch).astype(jnp.bfloat16)
    stream_wide = stream_out.astype(jnp.float32)
    inverse_rms = lax.rsqrt(lax.optimization_barrier(jnp.mean(stream_wide * stream_wide, axis=1, keepdims=True)) + EPSILON)
    normed = (stream_wide * inverse_rms * li_gain.astype(jnp.float32)[None]).astype(jnp.bfloat16)
    width_d = normed.shape[1]
    li_proj = jnp.dot(normed, li_in.reshape(width_d, 3 * width_d), preferred_element_type=jnp.float32)
    li_proj = li_proj.reshape(-1, 3, width_d).astype(jnp.bfloat16)
    li_mixed = short_filter(li_proj.astype(jnp.float32), li_short.astype(jnp.float32))
    li_values = (li_mixed[:, 1] * li_mixed[:, 2]).astype(jnp.bfloat16)
    li_filtered = modal_long_filter(li_values.astype(jnp.float32), li_res.astype(jnp.float32), li_rate.astype(jnp.float32), li_skip.astype(jnp.float32))
    li_output = (li_mixed[:, 0].T * li_filtered).astype(jnp.bfloat16)
    return (stream_out, li_output)
```

```python
import jax
import jax.numpy as jnp
from jax import lax
from jax.sharding import PartitionSpec as P

GROUP = 16


EPSILON = 1e-06
HIGHEST = lax.Precision.HIGHEST


def passed_along(block, axis, distance):
    devices = range(lax.axis_size(axis))
    route = [(i - distance, i) for i in devices if i - distance in devices]
    return lax.ppermute(block, axis, route)


def band_matrices(filters):
    tap_count = filters.shape[1]
    out_index = jnp.arange(tap_count, dtype=jnp.int32)[:, None, None]
    in_index = jnp.arange(2 * tap_count, dtype=jnp.int32)[None, :, None]
    lag_index = jnp.arange(tap_count, dtype=jnp.int32)[None, None, :]
    selector = (out_index + tap_count - 1 - in_index == lag_index).astype(jnp.bfloat16)
    return jnp.einsum(
        "gj,isj->gis", filters.astype(jnp.bfloat16), selector, preferred_element_type=jnp.float32
    ).astype(jnp.bfloat16)


def lagged_rows(extended, weights, row_count):
    running = weights[:, 0][None] * extended[2 : 2 + row_count]
    for lag_index in (1, 2):
        running = (
            running
            + weights[:, lag_index][None] * extended[2 - lag_index : 2 - lag_index + row_count]
        )
    return running


def swapped(blocks, axis):
    count = lax.axis_size(axis)
    if count != 2:
        return lax.all_to_all(blocks, axis, split_axis=0, concat_axis=0, tiled=True)
    me = lax.axis_index(axis)
    mine = lax.dynamic_index_in_dim(blocks, me, 0, keepdims=False)
    other = lax.dynamic_index_in_dim(blocks, 1 - me, 0, keepdims=False)
    received = lax.ppermute(other, axis, [(0, 1), (1, 0)])
    first = me == 0
    return jnp.stack([jnp.where(first, mine, received), jnp.where(first, received, mine)])


def summed_rows(blocks, axis):
    count = lax.axis_size(axis)
    if count != 2:
        return lax.psum_scatter(blocks.astype(jnp.bfloat16), axis, scatter_dimension=0).astype(
            jnp.float32
        )
    me = lax.axis_index(axis)
    mine = lax.dynamic_index_in_dim(blocks, me, 0, keepdims=False)
    other = lax.dynamic_index_in_dim(blocks, 1 - me, 0, keepdims=False).astype(jnp.bfloat16)
    return mine + lax.ppermute(other, axis, [(0, 1), (1, 0)]).astype(jnp.float32)


def modal_filter(values, residues, rates, skip_gain):
    chan_count, seq_length = values.shape
    size = min(128, seq_length)
    count = seq_length // size
    blocks_in = values.reshape(chan_count, count, size)
    lags = jnp.arange(size, dtype=jnp.float32)
    rising = residues[:, :, None] * jnp.exp(-rates[:, :, None] * lags)
    falling = jnp.exp(rates[:, :, None] * lags)
    product = jnp.einsum("rci,rcj->cij", rising, falling, precision=lax.Precision.HIGH)
    lower = (lags[:, None] >= lags[None, :])[None]
    matrix = jnp.where(lower, product, 0.0)
    matrix = matrix + jnp.where(
        lags[:, None] == lags[None, :], skip_gain[:, None, None], 0.0
    )
    within = jnp.einsum(
        "cij,cbj->cbi", matrix.astype(jnp.bfloat16), blocks_in, preferred_element_type=jnp.float32
    )
    ending = jnp.exp(-rates[:, :, None] * (size - 1.0 - lags)).astype(jnp.bfloat16)
    ends = jnp.einsum("rcj,cbj->rbc", ending, blocks_in, preferred_element_type=jnp.float32)
    index = jnp.arange(count, dtype=jnp.float32)
    apart = index[:, None] - 1.0 - index[None, :]
    decay = jnp.where(
        (apart >= 0.0)[None, :, :, None],
        jnp.exp(-rates[:, None, None, :] * size * jnp.maximum(apart, 0.0)[None, :, :, None]),
        0.0,
    )
    entering = jnp.sum(decay * ends[:, None], axis=2)
    rise_decay = residues[:, :, None] * jnp.exp(-rates[:, :, None] * (lags + 1.0))
    before = jnp.einsum(
        "rci,rbc->cbi",
        rise_decay.astype(jnp.bfloat16),
        entering.astype(jnp.bfloat16),
        preferred_element_type=jnp.float32,
    )
    return (within + before).reshape(chan_count, seq_length)


def lagged_time(rows, weights):
    length = rows.shape[1]
    padded = jnp.concatenate([jnp.zeros_like(rows[:, :2]), rows], axis=1).astype(jnp.float32)
    running = weights[0][:, None] * padded[:, 2:]
    for lag_index in (1, 2):
        running = running + weights[lag_index][:, None] * padded[:, 2 - lag_index : 2 - lag_index + length]
    return running


def local(
    stream_in,
    mr_proj,
    mr_short,
    mr_filter,
    mr_out,
    li_gain,
    li_in,
    li_short,
    li_res,
    li_rate,
    li_skip,
):
    row_count = mr_proj.shape[0]
    chan_width = mr_proj.shape[2]
    tap_count = mr_filter.shape[1]
    filter_count = mr_filter.shape[0]
    seq_size = lax.axis_size("seq")
    chan_size = lax.axis_size("chan")
    width = stream_in.shape[1]
    own_count = chan_width // seq_size
    part = row_count // chan_size
    me = lax.axis_index("chan")

    out_weights = lax.all_gather(mr_out.T, "seq", axis=0, tiled=True)

    in_blocks = li_in.reshape(li_in.shape[0], 3, seq_size, own_count)
    in_own = lax.all_to_all(
        jnp.transpose(in_blocks, (2, 1, 0, 3)), "seq", split_axis=0, concat_axis=0, tiled=True
    )
    in_own = jnp.transpose(in_own, (1, 0, 2, 3)).reshape(3, width, own_count)
    if chan_size == 2:
        in_other = lax.ppermute(in_own, "chan", [(0, 1), (1, 0)])
        first = me == 0
        in_all = jnp.stack(
            [jnp.where(first, in_own, in_other), jnp.where(first, in_other, in_own)]
        )
    else:
        in_all = lax.all_gather(in_own, "chan", axis=0)

    rim_rows = passed_along(mr_proj[-2:], "seq", 1)
    mr_mixed = lagged_rows(
        jnp.concatenate([rim_rows, mr_proj], axis=0).astype(jnp.float32), mr_short, row_count
    )
    queries = mr_mixed[:, 0]
    own_values = (mr_mixed[:, 1] * mr_mixed[:, 2]).astype(jnp.bfloat16)
    tail_rows = passed_along(own_values[-(tap_count - 1) :], "seq", 1)
    block_count = row_count // tap_count
    padded = jnp.concatenate(
        [tail_rows, own_values, jnp.zeros((1, chan_width), jnp.bfloat16)], axis=0
    )
    columns_major = padded.T.reshape(filter_count, GROUP, block_count + 1, tap_count)
    band_matrix = band_matrices(mr_filter)
    filtered_mr = jnp.einsum(
        "gis,gcbs->gcbi",
        band_matrix[:, :, :tap_count],
        columns_major[:, :, :-1],
        preferred_element_type=jnp.float32,
    )
    filtered_mr = filtered_mr + jnp.einsum(
        "gis,gcbs->gcbi",
        band_matrix[:, :, tap_count:],
        columns_major[:, :, 1:],
        preferred_element_type=jnp.float32,
    )
    filtered_rows = filtered_mr.reshape(chan_width, row_count).T
    gated = (queries * filtered_rows).astype(jnp.bfloat16)
    branch = jnp.einsum("tc,nc->tn", gated, out_weights, preferred_element_type=jnp.float32)
    summed = summed_rows(branch.reshape(chan_size, part, width), "chan")
    own_stream = lax.dynamic_slice_in_dim(stream_in, me * part, part, 0)
    stream = (own_stream.astype(jnp.float32) + summed).astype(jnp.bfloat16)
    stream_out = swapped(
        jnp.moveaxis(stream.reshape(part, chan_size, chan_width), 1, 0), "chan"
    ).reshape(row_count, chan_width)
    stream_wide = stream.astype(jnp.float32)
    inverse_rms = lax.rsqrt(jnp.mean(stream_wide * stream_wide, axis=1, keepdims=True) + EPSILON)
    normed = (stream_wide * inverse_rms * li_gain[None]).astype(jnp.bfloat16)
    gathered = lax.all_gather(normed, "seq", axis=0, tiled=True)

    def project(index):
        raw = jnp.einsum(
            "xdc,td->xct", in_all[:, index], gathered, preferred_element_type=jnp.float32
        ).astype(jnp.bfloat16)
        raw = swapped(raw, "chan").reshape(chan_size, own_count, seq_size, part)
        return jnp.transpose(raw, (1, 2, 0, 3)).reshape(own_count, seq_size * row_count)

    keys, gates, openers = project(1), project(2), project(0)
    seq_offset = lax.axis_index("seq") * own_count
    own_short = lax.dynamic_slice_in_dim(li_short, seq_offset, own_count, 2)
    own_res = lax.dynamic_slice_in_dim(li_res, seq_offset, own_count, 1)
    own_rate = lax.dynamic_slice_in_dim(li_rate, seq_offset, own_count, 1)
    own_skip = lax.dynamic_slice_in_dim(li_skip, seq_offset, own_count, 0)
    values = (lagged_time(keys, own_short[1]) * lagged_time(gates, own_short[2])).astype(
        jnp.bfloat16
    )
    filtered = modal_filter(values, own_res, own_rate, own_skip)
    result = (lagged_time(openers, own_short[0]) * filtered).astype(jnp.bfloat16)
    li_output = lax.all_to_all(result, "seq", split_axis=1, concat_axis=0, tiled=True)
    return (stream_out, li_output)


def solution(mesh):
    in_specs = (
        P("seq", None),
        P("seq", None, "chan"),
        P(None, None, "chan"),
        P("chan", None),
        P("chan", "seq"),
        P(),
        P("seq", None, "chan"),
        P(None, None, "chan"),
        P(None, "chan"),
        P(None, "chan"),
        P("chan"),
    )
    out_specs = (P("seq", "chan"), P("chan", "seq"))
    return jax.shard_map(local, mesh=mesh, in_specs=in_specs, out_specs=out_specs, check_vma=False)
```

```python
import jax
import jax.numpy as jnp
from jax import lax
from jax.sharding import PartitionSpec as P

GROUP = 16


EPSILON = 1e-06
HIGHEST = lax.Precision.HIGHEST


def passed_along(block, axis, distance):
    devices = range(lax.axis_size(axis))
    route = [(i - distance, i) for i in devices if i - distance in devices]
    return lax.ppermute(block, axis, route)


def band_matrices(filters):
    tap_count = filters.shape[1]
    out_index = jnp.arange(tap_count, dtype=jnp.int32)[:, None, None]
    in_index = jnp.arange(2 * tap_count, dtype=jnp.int32)[None, :, None]
    lag_index = jnp.arange(tap_count, dtype=jnp.int32)[None, None, :]
    selector = (out_index + tap_count - 1 - in_index == lag_index).astype(jnp.bfloat16)
    return jnp.einsum(
        "gj,isj->gis", filters.astype(jnp.bfloat16), selector, preferred_element_type=jnp.float32
    ).astype(jnp.bfloat16)


def lagged_rows(extended, weights, row_count):
    running = weights[:, 0][None] * extended[2 : 2 + row_count]
    for lag_index in (1, 2):
        running = (
            running
            + weights[:, lag_index][None] * extended[2 - lag_index : 2 - lag_index + row_count]
        )
    return running


def swapped(blocks, axis):
    count = lax.axis_size(axis)
    if count != 2:
        return lax.all_to_all(blocks, axis, split_axis=0, concat_axis=0, tiled=True)
    me = lax.axis_index(axis)
    mine = lax.dynamic_index_in_dim(blocks, me, 0, keepdims=False)
    other = lax.dynamic_index_in_dim(blocks, 1 - me, 0, keepdims=False)
    received = lax.ppermute(other, axis, [(0, 1), (1, 0)])
    first = me == 0
    return jnp.stack([jnp.where(first, mine, received), jnp.where(first, received, mine)])


def scattered(blocks, axis):
    count = lax.axis_size(axis)
    me = lax.axis_index(axis)
    pieces = []
    for k in range(count):
        block = lax.dynamic_index_in_dim(blocks, lax.rem(me + k, count), 0, keepdims=False)
        if k:
            block = lax.ppermute(block, axis, [(i, (i + k) % count) for i in range(count)])
        pieces.append(block)
    half = count // 2
    return jnp.stack(pieces[:half]), jnp.stack(pieces[half:])


def placed(first, second, axis):
    count = lax.axis_size(axis)
    me = lax.axis_index(axis)
    both = jnp.transpose(jnp.concatenate([first, second])[::-1], (0, 2, 1, 3))
    return lax.dynamic_slice_in_dim(
        jnp.concatenate([both, both]), lax.rem(2 * count - 1 - me, count), count, 0
    )


def summed_rows(blocks, axis):
    count = lax.axis_size(axis)
    if count != 2:
        return lax.psum_scatter(blocks.astype(jnp.bfloat16), axis, scatter_dimension=0).astype(
            jnp.float32
        )
    me = lax.axis_index(axis)
    mine = lax.dynamic_index_in_dim(blocks, me, 0, keepdims=False)
    other = lax.dynamic_index_in_dim(blocks, 1 - me, 0, keepdims=False).astype(jnp.bfloat16)
    return mine + lax.ppermute(other, axis, [(0, 1), (1, 0)]).astype(jnp.float32)


def modal_filter(values, residues, rates, skip_gain):
    chan_count, seq_length = values.shape
    size = min(128, seq_length)
    count = seq_length // size
    blocks_in = values.reshape(chan_count, count, size)
    lags = jnp.arange(size, dtype=jnp.float32)
    rising = residues[:, :, None] * jnp.exp(-rates[:, :, None] * lags)
    falling = jnp.exp(rates[:, :, None] * lags)
    product = jnp.einsum("rci,rcj->cij", rising, falling, precision=lax.Precision.HIGH)
    lower = (lags[:, None] >= lags[None, :])[None]
    matrix = jnp.where(lower, product, 0.0)
    matrix = matrix + jnp.where(
        lags[:, None] == lags[None, :], skip_gain[:, None, None], 0.0
    )
    within = jnp.einsum(
        "cij,cbj->cbi", matrix.astype(jnp.bfloat16), blocks_in, preferred_element_type=jnp.float32
    )
    ending = jnp.exp(-rates[:, :, None] * (size - 1.0 - lags)).astype(jnp.bfloat16)
    ends = jnp.einsum("rcj,cbj->rbc", ending, blocks_in, preferred_element_type=jnp.float32)
    index = jnp.arange(count, dtype=jnp.float32)
    apart = index[:, None] - 1.0 - index[None, :]
    decay = jnp.where(
        (apart >= 0.0)[None, :, :, None],
        jnp.exp(-rates[:, None, None, :] * size * jnp.maximum(apart, 0.0)[None, :, :, None]),
        0.0,
    )
    entering = jnp.sum(decay * ends[:, None], axis=2)
    rise_decay = residues[:, :, None] * jnp.exp(-rates[:, :, None] * (lags + 1.0))
    before = jnp.einsum(
        "rci,rbc->cbi",
        rise_decay.astype(jnp.bfloat16),
        entering.astype(jnp.bfloat16),
        preferred_element_type=jnp.float32,
    )
    return (within + before).reshape(chan_count, seq_length)


def lagged_time(rows, weights):
    length = rows.shape[1]
    padded = jnp.concatenate([jnp.zeros_like(rows[:, :2]), rows], axis=1).astype(jnp.float32)
    running = weights[0][:, None] * padded[:, 2:]
    for lag_index in (1, 2):
        running = running + weights[lag_index][:, None] * padded[:, 2 - lag_index : 2 - lag_index + length]
    return running


def local(
    stream_in,
    mr_proj,
    mr_short,
    mr_filter,
    mr_out,
    li_gain,
    li_in,
    li_short,
    li_res,
    li_rate,
    li_skip,
):
    row_count = mr_proj.shape[0]
    chan_width = mr_proj.shape[2]
    tap_count = mr_filter.shape[1]
    filter_count = mr_filter.shape[0]
    seq_size = lax.axis_size("seq")
    chan_size = lax.axis_size("chan")
    width = stream_in.shape[1]
    own_count = chan_width // seq_size
    part = row_count // chan_size
    me = lax.axis_index("chan")

    out_weights = lax.all_gather(mr_out, "seq", axis=0)

    in_blocks = jnp.transpose(
        li_in.reshape(li_in.shape[0], 3, seq_size, own_count), (2, 1, 0, 3)
    )
    in_first, in_second = scattered(in_blocks, "seq")

    rim_rows = passed_along(mr_proj[-2:], "seq", 1)
    mr_mixed = lagged_rows(
        jnp.concatenate([rim_rows, mr_proj], axis=0).astype(jnp.float32), mr_short, row_count
    )
    queries = mr_mixed[:, 0]
    own_values = (mr_mixed[:, 1] * mr_mixed[:, 2]).astype(jnp.bfloat16)
    tail_rows = passed_along(own_values[-(tap_count - 1) :], "seq", 1)
    block_count = row_count // tap_count
    padded = jnp.concatenate(
        [tail_rows, own_values, jnp.zeros((1, chan_width), jnp.bfloat16)], axis=0
    )
    columns_major = padded.T.reshape(filter_count, GROUP, block_count + 1, tap_count)
    band_matrix = band_matrices(mr_filter)
    filtered_mr = jnp.einsum(
        "gis,gcbs->gcbi",
        band_matrix[:, :, :tap_count],
        columns_major[:, :, :-1],
        preferred_element_type=jnp.float32,
    )
    filtered_mr = filtered_mr + jnp.einsum(
        "gis,gcbs->gcbi",
        band_matrix[:, :, tap_count:],
        columns_major[:, :, 1:],
        preferred_element_type=jnp.float32,
    )
    filtered_rows = filtered_mr.reshape(chan_width, row_count).T
    gated = (queries * filtered_rows).astype(jnp.bfloat16)
    gated, in_first, in_second = lax.optimization_barrier((gated, in_first, in_second))
    branch = jnp.einsum("tc,scn->tsn", gated, out_weights, preferred_element_type=jnp.float32)
    summed = summed_rows(branch.reshape(chan_size, part, width), "chan")
    own_stream = lax.dynamic_slice_in_dim(stream_in, me * part, part, 0)
    stream = (own_stream.astype(jnp.float32) + summed).astype(jnp.bfloat16)
    stream_out = swapped(
        jnp.moveaxis(stream.reshape(part, chan_size, chan_width), 1, 0), "chan"
    ).reshape(row_count, chan_width)
    stream_wide = stream.astype(jnp.float32)
    inverse_rms = lax.rsqrt(jnp.mean(stream_wide * stream_wide, axis=1, keepdims=True) + EPSILON)
    normed = (stream_wide * inverse_rms * li_gain[None]).astype(jnp.bfloat16)
    normed, in_first, in_second = lax.optimization_barrier((normed, in_first, in_second))
    gathered = lax.all_gather(normed, "seq", axis=0, tiled=True)
    in_own = placed(in_first, in_second, "seq").reshape(width, 3 * own_count)
    if chan_size == 2:
        swap = [(0, 1), (1, 0)]
        in_other = placed(
            lax.ppermute(in_first, "chan", swap), lax.ppermute(in_second, "chan", swap), "seq"
        ).reshape(width, 3 * own_count)
        gathered, stream_out = lax.optimization_barrier((gathered, stream_out))

        def product(matrix, low, high):
            return jnp.dot(
                gathered,
                matrix[:, low * own_count : high * own_count],
                preferred_element_type=jnp.float32,
            ).astype(jnp.bfloat16)

        sent = lax.ppermute(product(in_other, 1, 3), "chan", swap)
        sent_opener = lax.ppermute(product(in_other, 0, 1), "chan", swap)
        kept = product(in_own, 0, 3)
        received = (sent_opener, sent[:, :own_count], sent[:, own_count:])

        def ordered(index):
            mine = kept[:, index * own_count : (index + 1) * own_count].T
            theirs = received[index].T
            pair = [
                jnp.where(me == 0, mine, theirs).reshape(own_count, seq_size, 1, part),
                jnp.where(me == 0, theirs, mine).reshape(own_count, seq_size, 1, part),
            ]
            return jnp.concatenate(pair, axis=2).reshape(own_count, seq_size * row_count)
    else:
        in_all = lax.all_gather(in_own, "chan", axis=0)
        raw = jnp.einsum(
            "xdn,td->xnt", in_all, gathered, preferred_element_type=jnp.float32
        ).astype(jnp.bfloat16)
        raw = swapped(raw, "chan").reshape(chan_size, 3, own_count, seq_size, part)
        raw = jnp.transpose(raw, (1, 2, 3, 0, 4)).reshape(3, own_count, seq_size * row_count)

        def ordered(index):
            return raw[index]

    keys, gates, openers = ordered(1), ordered(2), ordered(0)
    seq_offset = lax.axis_index("seq") * own_count
    own_short = lax.dynamic_slice_in_dim(li_short, seq_offset, own_count, 2)
    own_res = lax.dynamic_slice_in_dim(li_res, seq_offset, own_count, 1)
    own_rate = lax.dynamic_slice_in_dim(li_rate, seq_offset, own_count, 1)
    own_skip = lax.dynamic_slice_in_dim(li_skip, seq_offset, own_count, 0)
    values = (lagged_time(keys, own_short[1]) * lagged_time(gates, own_short[2])).astype(
        jnp.bfloat16
    )
    filtered = modal_filter(values, own_res, own_rate, own_skip)
    result = (lagged_time(openers, own_short[0]) * filtered).astype(jnp.bfloat16)
    li_output = lax.all_to_all(result, "seq", split_axis=1, concat_axis=0, tiled=True)
    return (stream_out, li_output)


def solution(mesh):
    in_specs = (
        P("seq", None),
        P("seq", None, "chan"),
        P(None, None, "chan"),
        P("chan", None),
        P("chan", "seq"),
        P(),
        P("seq", None, "chan"),
        P(None, None, "chan"),
        P(None, "chan"),
        P(None, "chan"),
        P("chan"),
    )
    out_specs = (P("seq", "chan"), P("chan", "seq"))
    return jax.shard_map(local, mesh=mesh, in_specs=in_specs, out_specs=out_specs, check_vma=False)
```

```python
import functools

import jax
import jax.numpy as jnp
from jax import lax
from jax.experimental import pallas as pl
from jax.experimental.pallas import tpu as pltpu
from jax.sharding import PartitionSpec as P

GROUP = 16


EPSILON = 1e-06
HIGHEST = lax.Precision.HIGHEST


def passed_along(block, axis, distance):
    devices = range(lax.axis_size(axis))
    route = [(i - distance, i) for i in devices if i - distance in devices]
    return lax.ppermute(block, axis, route)


def band_matrices(filters):
    tap_count = filters.shape[1]
    out_index = jnp.arange(tap_count, dtype=jnp.int32)[:, None, None]
    in_index = jnp.arange(2 * tap_count, dtype=jnp.int32)[None, :, None]
    lag_index = jnp.arange(tap_count, dtype=jnp.int32)[None, None, :]
    selector = (out_index + tap_count - 1 - in_index == lag_index).astype(jnp.bfloat16)
    return jnp.einsum(
        "gj,isj->gis", filters.astype(jnp.bfloat16), selector, preferred_element_type=jnp.float32
    ).astype(jnp.bfloat16)


def lagged_rows(extended, weights, row_count):
    running = weights[:, 0][None] * extended[2 : 2 + row_count]
    for lag_index in (1, 2):
        running = (
            running
            + weights[:, lag_index][None] * extended[2 - lag_index : 2 - lag_index + row_count]
        )
    return running


def swapped(blocks, axis):
    count = lax.axis_size(axis)
    if count != 2:
        return lax.all_to_all(blocks, axis, split_axis=0, concat_axis=0, tiled=True)
    me = lax.axis_index(axis)
    mine = lax.dynamic_index_in_dim(blocks, me, 0, keepdims=False)
    other = lax.dynamic_index_in_dim(blocks, 1 - me, 0, keepdims=False)
    received = lax.ppermute(other, axis, [(0, 1), (1, 0)])
    first = me == 0
    return jnp.stack([jnp.where(first, mine, received), jnp.where(first, received, mine)])


def scattered(blocks, axis):
    count = lax.axis_size(axis)
    me = lax.axis_index(axis)
    pieces = []
    for k in range(count):
        block = lax.dynamic_index_in_dim(blocks, lax.rem(me + k, count), 0, keepdims=False)
        if k:
            block = lax.ppermute(block, axis, [(i, (i + k) % count) for i in range(count)])
        pieces.append(block)
    half = count // 2
    return jnp.stack(pieces[:half]), jnp.stack(pieces[half:])


def placed(first, second, axis):
    count = lax.axis_size(axis)
    me = lax.axis_index(axis)
    both = jnp.transpose(jnp.concatenate([first, second])[::-1], (0, 2, 1, 3))
    return lax.dynamic_slice_in_dim(
        jnp.concatenate([both, both]), lax.rem(2 * count - 1 - me, count), count, 0
    )


PARTS = 4


def ring_kernel(chips, swaps, *refs):
    inputs, outputs, sems = refs[: 1 + swaps], refs[1 + swaps : 2 + 2 * swaps], refs[2 + 2 * swaps :]
    block_ref, out_ref = inputs[0], outputs[0]
    ring_send, ring_recv, core_send, core_recv, own_sem, swap_send, swap_recv = sems
    me = lax.axis_index("seq")
    core = lax.rem(me, 2)
    chip = me // 2
    row, column = chip // 2, lax.rem(chip, 2)
    place = row + column * (chips - 1 - 2 * row)
    sibling = me + 1 - 2 * core
    rows = block_ref.shape[0] // PARTS

    def device(position, core_index):
        position = lax.rem(position + 2 * chips, chips)
        second = position // (chips // 2)
        at_row = position + second * (chips - 1 - 2 * position)
        return (2 * at_row + second) * 2 + core_index

    following, preceding = device(place + 1, core), device(place - 1, core)
    barrier = pltpu.get_barrier_semaphore()
    for target in (following, preceding, sibling):
        pl.semaphore_signal(barrier, inc=1, device_id={"seq": target})
    if swaps:
        partner = 1 - lax.axis_index("chan")
        pl.semaphore_signal(barrier, inc=1, device_id={"chan": partner})
    pl.semaphore_wait(barrier, 4 if swaps else 3)

    def ring(way, step, half, source, slot):
        part = pl.ds((2 * way + half) * rows, rows)
        index = (way * (chips - 1) + step) * 2 + half
        return pltpu.make_async_remote_copy(
            src_ref=source.at[part],
            dst_ref=out_ref.at[slot, part],
            send_sem=ring_send.at[index],
            recv_sem=ring_recv.at[index],
            device_id={"seq": (following, preceding)[way]},
        )

    def across(way, step, half, source, slot):
        part = pl.ds((2 * way + half) * rows, rows)
        index = (way * chips + step) * 2 + half
        return pltpu.make_async_remote_copy(
            src_ref=source.at[part],
            dst_ref=out_ref.at[slot, part],
            send_sem=core_send.at[index],
            recv_sem=core_recv.at[index],
            device_id={"seq": sibling},
        )

    started = []
    for step in range(chips):
        for half in (0, 1):
            for way in (0, 1):
                slot = device(place + (2 * way - 1) * step, core)
                source = block_ref if step == 0 else out_ref.at[slot]
                if step:
                    ring(way, step - 1, half, source, slot).wait_recv()
                if step < chips - 1:
                    copy = ring(way, step, half, source, slot)
                    copy.start()
                    started.append(copy)
                copy = across(way, step, half, source, slot)
                copy.start()
                started.append(copy)
        if step == 0:
            for i in range(swaps):
                copy = pltpu.make_async_remote_copy(
                    src_ref=inputs[1 + i],
                    dst_ref=outputs[1 + i],
                    send_sem=swap_send.at[i],
                    recv_sem=swap_recv.at[i],
                    device_id={"chan": partner},
                )
                copy.start()
                started.append(copy)
            own = pltpu.make_async_copy(block_ref, out_ref.at[me], own_sem)
            own.start()
    for step in range(chips):
        for half in (0, 1):
            for way in (0, 1):
                slot = device(place + (2 * way - 1) * step, 1 - core)
                across(way, step, half, out_ref.at[slot], slot).wait_recv()
    own.wait()
    for copy in started:
        copy.wait_send()
    for i in range(swaps):
        pltpu.make_async_remote_copy(
            src_ref=inputs[1 + i],
            dst_ref=outputs[1 + i],
            send_sem=swap_send.at[i],
            recv_sem=swap_recv.at[i],
            device_id={"chan": partner},
        ).wait_recv()


def gathered_rows(block, *swapped_arrays):
    seq_size = lax.axis_size("seq")
    chips = seq_size // 2
    swaps = len(swapped_arrays)
    dma = pltpu.SemaphoreType.DMA
    results = pl.pallas_call(
        functools.partial(ring_kernel, chips, swaps),
        out_shape=[jax.ShapeDtypeStruct((seq_size,) + block.shape, block.dtype)]
        + [jax.ShapeDtypeStruct(a.shape, a.dtype) for a in swapped_arrays],
        in_specs=[pl.BlockSpec(memory_space=pl.ANY)] * (1 + swaps),
        out_specs=[pl.BlockSpec(memory_space=pl.ANY)] * (1 + swaps),
        scratch_shapes=[
            dma((4 * (chips - 1),)),
            dma((4 * (chips - 1),)),
            dma((4 * chips,)),
            dma((4 * chips,)),
            dma,
            dma((max(swaps, 1),)),
            dma((max(swaps, 1),)),
        ],
        compiler_params=pltpu.CompilerParams(collective_id=0, has_side_effects=True),
    )(block, *swapped_arrays)
    return [results[0].reshape(seq_size * block.shape[0], block.shape[1])] + list(results[1:])


def summed_rows(blocks, axis):
    count = lax.axis_size(axis)
    if count != 2:
        return lax.psum_scatter(blocks.astype(jnp.bfloat16), axis, scatter_dimension=0).astype(
            jnp.float32
        )
    me = lax.axis_index(axis)
    mine = lax.dynamic_index_in_dim(blocks, me, 0, keepdims=False)
    other = lax.dynamic_index_in_dim(blocks, 1 - me, 0, keepdims=False).astype(jnp.bfloat16)
    return mine + lax.ppermute(other, axis, [(0, 1), (1, 0)]).astype(jnp.float32)


def modal_filter(values, residues, rates, skip_gain):
    chan_count, seq_length = values.shape
    size = min(128, seq_length)
    count = seq_length // size
    blocks_in = values.reshape(chan_count, count, size)
    lags = jnp.arange(size, dtype=jnp.float32)
    rising = residues[:, :, None] * jnp.exp(-rates[:, :, None] * lags)
    falling = jnp.exp(rates[:, :, None] * lags)
    product = jnp.einsum("rci,rcj->cij", rising, falling, precision=lax.Precision.HIGH)
    lower = (lags[:, None] >= lags[None, :])[None]
    matrix = jnp.where(lower, product, 0.0)
    matrix = matrix + jnp.where(
        lags[:, None] == lags[None, :], skip_gain[:, None, None], 0.0
    )
    within = jnp.einsum(
        "cij,cbj->cbi", matrix.astype(jnp.bfloat16), blocks_in, preferred_element_type=jnp.float32
    )
    ending = jnp.exp(-rates[:, :, None] * (size - 1.0 - lags)).astype(jnp.bfloat16)
    ends = jnp.einsum("rcj,cbj->rbc", ending, blocks_in, preferred_element_type=jnp.float32)
    index = jnp.arange(count, dtype=jnp.float32)
    apart = index[:, None] - 1.0 - index[None, :]
    decay = jnp.where(
        (apart >= 0.0)[None, :, :, None],
        jnp.exp(-rates[:, None, None, :] * size * jnp.maximum(apart, 0.0)[None, :, :, None]),
        0.0,
    )
    entering = jnp.sum(decay * ends[:, None], axis=2)
    rise_decay = residues[:, :, None] * jnp.exp(-rates[:, :, None] * (lags + 1.0))
    before = jnp.einsum(
        "rci,rbc->cbi",
        rise_decay.astype(jnp.bfloat16),
        entering.astype(jnp.bfloat16),
        preferred_element_type=jnp.float32,
    )
    return (within + before).reshape(chan_count, seq_length)


def lagged_time(rows, weights):
    length = rows.shape[1]
    padded = jnp.concatenate([jnp.zeros_like(rows[:, :2]), rows], axis=1).astype(jnp.float32)
    running = weights[0][:, None] * padded[:, 2:]
    for lag_index in (1, 2):
        running = running + weights[lag_index][:, None] * padded[:, 2 - lag_index : 2 - lag_index + length]
    return running


def local(
    stream_in,
    mr_proj,
    mr_short,
    mr_filter,
    mr_out,
    li_gain,
    li_in,
    li_short,
    li_res,
    li_rate,
    li_skip,
):
    row_count = mr_proj.shape[0]
    chan_width = mr_proj.shape[2]
    tap_count = mr_filter.shape[1]
    filter_count = mr_filter.shape[0]
    seq_size = lax.axis_size("seq")
    chan_size = lax.axis_size("chan")
    width = stream_in.shape[1]
    own_count = chan_width // seq_size
    part = row_count // chan_size
    me = lax.axis_index("chan")

    out_weights = lax.all_gather(mr_out, "seq", axis=0)

    in_blocks = jnp.transpose(
        li_in.reshape(li_in.shape[0], 3, seq_size, own_count), (2, 1, 0, 3)
    )
    in_own = placed(*scattered(in_blocks, "seq"), "seq").reshape(width, 3 * own_count)

    rim_rows = passed_along(mr_proj[-2:], "seq", 1)
    mr_mixed = lagged_rows(
        jnp.concatenate([rim_rows, mr_proj], axis=0).astype(jnp.float32), mr_short, row_count
    )
    queries = mr_mixed[:, 0]
    own_values = (mr_mixed[:, 1] * mr_mixed[:, 2]).astype(jnp.bfloat16)
    tail_rows = passed_along(own_values[-(tap_count - 1) :], "seq", 1)
    block_count = row_count // tap_count
    padded = jnp.concatenate(
        [tail_rows, own_values, jnp.zeros((1, chan_width), jnp.bfloat16)], axis=0
    )
    columns_major = padded.T.reshape(filter_count, GROUP, block_count + 1, tap_count)
    band_matrix = band_matrices(mr_filter)
    filtered_mr = jnp.einsum(
        "gis,gcbs->gcbi",
        band_matrix[:, :, :tap_count],
        columns_major[:, :, :-1],
        preferred_element_type=jnp.float32,
    )
    filtered_mr = filtered_mr + jnp.einsum(
        "gis,gcbs->gcbi",
        band_matrix[:, :, tap_count:],
        columns_major[:, :, 1:],
        preferred_element_type=jnp.float32,
    )
    filtered_rows = filtered_mr.reshape(chan_width, row_count).T
    gated = (queries * filtered_rows).astype(jnp.bfloat16)
    gated, in_own = lax.optimization_barrier((gated, in_own))
    branch = jnp.einsum("tc,scn->tsn", gated, out_weights, preferred_element_type=jnp.float32)
    summed = summed_rows(branch.reshape(chan_size, part, width), "chan")
    own_stream = lax.dynamic_slice_in_dim(stream_in, me * part, part, 0)
    stream = (own_stream.astype(jnp.float32) + summed).astype(jnp.bfloat16)
    stream_wide = stream.astype(jnp.float32)
    inverse_rms = lax.rsqrt(jnp.mean(stream_wide * stream_wide, axis=1, keepdims=True) + EPSILON)
    normed = (stream_wide * inverse_rms * li_gain[None]).astype(jnp.bfloat16)
    stream_parts = jnp.moveaxis(stream.reshape(part, chan_size, chan_width), 1, 0)
    if chan_size == 2:
        swap = [(0, 1), (1, 0)]
        stream_mine = lax.dynamic_index_in_dim(stream_parts, me, 0, keepdims=False)
        stream_other = lax.dynamic_index_in_dim(stream_parts, 1 - me, 0, keepdims=False)
        gathered, in_other, stream_other = gathered_rows(normed, in_own, stream_other)
        stream_out = jnp.concatenate(
            [
                jnp.where(me == 0, stream_mine, stream_other),
                jnp.where(me == 0, stream_other, stream_mine),
            ]
        )

        def product(matrix, low, high):
            return jnp.dot(
                gathered,
                matrix[:, low * own_count : high * own_count],
                preferred_element_type=jnp.float32,
            ).astype(jnp.bfloat16)

        sent = lax.ppermute(product(in_other, 1, 3), "chan", swap)
        sent_opener = lax.ppermute(product(in_other, 0, 1), "chan", swap)
        kept = product(in_own, 0, 3)
        received = (sent_opener, sent[:, :own_count], sent[:, own_count:])

        def ordered(index):
            mine = kept[:, index * own_count : (index + 1) * own_count].T
            theirs = received[index].T
            pair = [
                jnp.where(me == 0, mine, theirs).reshape(own_count, seq_size, 1, part),
                jnp.where(me == 0, theirs, mine).reshape(own_count, seq_size, 1, part),
            ]
            return jnp.concatenate(pair, axis=2).reshape(own_count, seq_size * row_count)
    else:
        stream_out = swapped(stream_parts, "chan").reshape(row_count, chan_width)
        gathered = gathered_rows(normed)[0]
        in_all = lax.all_gather(in_own, "chan", axis=0)
        raw = jnp.einsum(
            "xdn,td->xnt", in_all, gathered, preferred_element_type=jnp.float32
        ).astype(jnp.bfloat16)
        raw = swapped(raw, "chan").reshape(chan_size, 3, own_count, seq_size, part)
        raw = jnp.transpose(raw, (1, 2, 3, 0, 4)).reshape(3, own_count, seq_size * row_count)

        def ordered(index):
            return raw[index]

    keys, gates, openers = ordered(1), ordered(2), ordered(0)
    seq_offset = lax.axis_index("seq") * own_count
    own_short = lax.dynamic_slice_in_dim(li_short, seq_offset, own_count, 2)
    own_res = lax.dynamic_slice_in_dim(li_res, seq_offset, own_count, 1)
    own_rate = lax.dynamic_slice_in_dim(li_rate, seq_offset, own_count, 1)
    own_skip = lax.dynamic_slice_in_dim(li_skip, seq_offset, own_count, 0)
    values = (lagged_time(keys, own_short[1]) * lagged_time(gates, own_short[2])).astype(
        jnp.bfloat16
    )
    filtered = modal_filter(values, own_res, own_rate, own_skip)
    result = (lagged_time(openers, own_short[0]) * filtered).astype(jnp.bfloat16)
    li_output = lax.all_to_all(result, "seq", split_axis=1, concat_axis=0, tiled=True)
    return (stream_out, li_output)


def solution(mesh):
    in_specs = (
        P("seq", None),
        P("seq", None, "chan"),
        P(None, None, "chan"),
        P("chan", None),
        P("chan", "seq"),
        P(),
        P("seq", None, "chan"),
        P(None, None, "chan"),
        P(None, "chan"),
        P(None, "chan"),
        P("chan"),
    )
    out_specs = (P("seq", "chan"), P("chan", "seq"))
    return jax.shard_map(local, mesh=mesh, in_specs=in_specs, out_specs=out_specs, check_vma=False)
```

```python
import functools

import jax
import jax.numpy as jnp
from jax import lax
from jax.experimental import pallas as pl
from jax.experimental.pallas import tpu as pltpu
from jax.sharding import PartitionSpec as P

GROUP = 16


EPSILON = 1e-06
HIGHEST = lax.Precision.HIGHEST


def passed_along(block, axis, distance):
    devices = range(lax.axis_size(axis))
    route = [(i - distance, i) for i in devices if i - distance in devices]
    return lax.ppermute(block, axis, route)


def band_matrices(filters):
    tap_count = filters.shape[1]
    out_index = jnp.arange(tap_count, dtype=jnp.int32)[:, None, None]
    in_index = jnp.arange(2 * tap_count, dtype=jnp.int32)[None, :, None]
    lag_index = jnp.arange(tap_count, dtype=jnp.int32)[None, None, :]
    selector = (out_index + tap_count - 1 - in_index == lag_index).astype(jnp.bfloat16)
    return jnp.einsum(
        "gj,isj->gis", filters.astype(jnp.bfloat16), selector, preferred_element_type=jnp.float32
    ).astype(jnp.bfloat16)


def lagged_rows(extended, weights, row_count):
    running = weights[:, 0][None] * extended[2 : 2 + row_count]
    for lag_index in (1, 2):
        running = (
            running
            + weights[:, lag_index][None] * extended[2 - lag_index : 2 - lag_index + row_count]
        )
    return running


def swapped(blocks, axis):
    count = lax.axis_size(axis)
    if count != 2:
        return lax.all_to_all(blocks, axis, split_axis=0, concat_axis=0, tiled=True)
    me = lax.axis_index(axis)
    mine = lax.dynamic_index_in_dim(blocks, me, 0, keepdims=False)
    other = lax.dynamic_index_in_dim(blocks, 1 - me, 0, keepdims=False)
    received = lax.ppermute(other, axis, [(0, 1), (1, 0)])
    first = me == 0
    return jnp.stack([jnp.where(first, mine, received), jnp.where(first, received, mine)])


def scattered(blocks, axis):
    count = lax.axis_size(axis)
    me = lax.axis_index(axis)
    chips, chip = count // 2, me // 2
    pairs = blocks.reshape((chips, 2) + blocks.shape[1:])
    pieces = []
    for k in range(chips):
        piece = lax.dynamic_index_in_dim(pairs, lax.rem(chip + k, chips), 0, keepdims=False)
        if k:
            route = [(i, (i + 2 * k) % count) for i in range(count)]
            piece = lax.ppermute(piece, axis, route)
        pieces.append(piece)
    return pieces


def assembled(pieces, axis):
    count = lax.axis_size(axis)
    me = lax.axis_index(axis)
    chips, chip, core = count // 2, me // 2, lax.rem(me, 2)
    kept = jnp.stack([lax.dynamic_index_in_dim(p, core, 0, keepdims=False) for p in pieces])
    given = jnp.stack([lax.dynamic_index_in_dim(p, 1 - core, 0, keepdims=False) for p in pieces])
    taken = lax.ppermute(given, axis, [(i, i ^ 1) for i in range(count)])
    both = jnp.stack(
        [jnp.where(core == 0, kept, taken), jnp.where(core == 0, taken, kept)], axis=1
    )
    both = jnp.transpose(both[::-1], (0, 1, 3, 2, 4))
    return lax.dynamic_slice_in_dim(
        jnp.concatenate([both, both]), lax.rem(2 * chips - 1 - chip, chips), chips, 0
    )


def branch_kernel(gated_ref, weights_ref, out_ref):
    out_ref[...] = jnp.dot(gated_ref[...], weights_ref[0], preferred_element_type=jnp.float32)


def branch_product(gated, weights):
    rows, depth = gated.shape
    blocks, _, columns = weights.shape
    return pl.pallas_call(
        branch_kernel,
        out_shape=jax.ShapeDtypeStruct((rows, blocks * columns), jnp.float32),
        grid=(blocks,),
        in_specs=[
            pl.BlockSpec((rows, depth), lambda i: (0, 0)),
            pl.BlockSpec((1, depth, columns), lambda i: (i, 0, 0)),
        ],
        out_specs=pl.BlockSpec((rows, columns), lambda i: (0, i)),
        cost_estimate=pl.CostEstimate(
            flops=2 * rows * depth * blocks * columns,
            bytes_accessed=2 * blocks * depth * columns,
            transcendentals=0,
        ),
    )(gated, weights)


PARTS = 4


def ring_kernel(chips, swaps, *refs):
    inputs, outputs, sems = refs[: 1 + swaps], refs[1 + swaps : 2 + 2 * swaps], refs[2 + 2 * swaps :]
    block_ref, out_ref = inputs[0], outputs[0]
    ring_send, ring_recv, core_send, core_recv, own_sem, swap_send, swap_recv = sems
    me = lax.axis_index("seq")
    core = lax.rem(me, 2)
    chip = me // 2
    row, column = chip // 2, lax.rem(chip, 2)
    place = row + column * (chips - 1 - 2 * row)
    sibling = me + 1 - 2 * core
    rows = block_ref.shape[0] // PARTS

    def device(position, core_index):
        position = lax.rem(position + 2 * chips, chips)
        second = position // (chips // 2)
        at_row = position + second * (chips - 1 - 2 * position)
        return (2 * at_row + second) * 2 + core_index

    following, preceding = device(place + 1, core), device(place - 1, core)
    barrier = pltpu.get_barrier_semaphore()
    for target in (following, preceding, sibling):
        pl.semaphore_signal(barrier, inc=1, device_id={"seq": target})
    if swaps:
        partner = 1 - lax.axis_index("chan")
        pl.semaphore_signal(barrier, inc=1, device_id={"chan": partner})
    pl.semaphore_wait(barrier, 4 if swaps else 3)

    def ring(way, step, half, source, slot):
        part = pl.ds((2 * way + half) * rows, rows)
        index = (way * (chips - 1) + step) * 2 + half
        return pltpu.make_async_remote_copy(
            src_ref=source.at[part],
            dst_ref=out_ref.at[slot, part],
            send_sem=ring_send.at[index],
            recv_sem=ring_recv.at[index],
            device_id={"seq": (following, preceding)[way]},
        )

    def across(way, step, half, source, slot):
        part = pl.ds((2 * way + half) * rows, rows)
        index = (way * chips + step) * 2 + half
        return pltpu.make_async_remote_copy(
            src_ref=source.at[part],
            dst_ref=out_ref.at[slot, part],
            send_sem=core_send.at[index],
            recv_sem=core_recv.at[index],
            device_id={"seq": sibling},
        )

    started = []
    for step in range(chips):
        for half in (0, 1):
            for way in (0, 1):
                slot = device(place + (2 * way - 1) * step, core)
                source = block_ref if step == 0 else out_ref.at[slot]
                if step:
                    ring(way, step - 1, half, source, slot).wait_recv()
                if step < chips - 1:
                    copy = ring(way, step, half, source, slot)
                    copy.start()
                    started.append(copy)
                copy = across(way, step, half, source, slot)
                copy.start()
                started.append(copy)
        if step == 0:
            for i in range(swaps):
                copy = pltpu.make_async_remote_copy(
                    src_ref=inputs[1 + i],
                    dst_ref=outputs[1 + i],
                    send_sem=swap_send.at[i],
                    recv_sem=swap_recv.at[i],
                    device_id={"chan": partner},
                )
                copy.start()
                started.append(copy)
            own = pltpu.make_async_copy(block_ref, out_ref.at[me], own_sem)
            own.start()
    for step in range(chips):
        for half in (0, 1):
            for way in (0, 1):
                slot = device(place + (2 * way - 1) * step, 1 - core)
                across(way, step, half, out_ref.at[slot], slot).wait_recv()
    own.wait()
    for copy in started:
        copy.wait_send()
    for i in range(swaps):
        pltpu.make_async_remote_copy(
            src_ref=inputs[1 + i],
            dst_ref=outputs[1 + i],
            send_sem=swap_send.at[i],
            recv_sem=swap_recv.at[i],
            device_id={"chan": partner},
        ).wait_recv()


def gathered_rows(identity, block, *swapped_arrays):
    seq_size = lax.axis_size("seq")
    chips = seq_size // 2
    swaps = len(swapped_arrays)
    dma = pltpu.SemaphoreType.DMA
    results = pl.pallas_call(
        functools.partial(ring_kernel, chips, swaps),
        out_shape=[jax.ShapeDtypeStruct((seq_size,) + block.shape, block.dtype)]
        + [jax.ShapeDtypeStruct(a.shape, a.dtype) for a in swapped_arrays],
        in_specs=[pl.BlockSpec(memory_space=pl.ANY)] * (1 + swaps),
        out_specs=[pl.BlockSpec(memory_space=pl.ANY)] * (1 + swaps),
        scratch_shapes=[
            dma((4 * (chips - 1),)),
            dma((4 * (chips - 1),)),
            dma((4 * chips,)),
            dma((4 * chips,)),
            dma,
            dma((max(swaps, 1),)),
            dma((max(swaps, 1),)),
        ],
        compiler_params=pltpu.CompilerParams(collective_id=identity, has_side_effects=True),
    )(block, *swapped_arrays)
    return results


def summed_rows(blocks, axis):
    count = lax.axis_size(axis)
    if count != 2:
        return lax.psum_scatter(blocks.astype(jnp.bfloat16), axis, scatter_dimension=0).astype(
            jnp.float32
        )
    me = lax.axis_index(axis)
    mine = lax.dynamic_index_in_dim(blocks, me, 0, keepdims=False)
    other = lax.dynamic_index_in_dim(blocks, 1 - me, 0, keepdims=False).astype(jnp.bfloat16)
    return mine + lax.ppermute(other, axis, [(0, 1), (1, 0)]).astype(jnp.float32)


def modal_filter(values, residues, rates, skip_gain):
    chan_count, seq_length = values.shape
    size = min(128, seq_length)
    count = seq_length // size
    blocks_in = values.reshape(chan_count, count, size)
    lags = jnp.arange(size, dtype=jnp.float32)
    rising = residues[:, :, None] * jnp.exp(-rates[:, :, None] * lags)
    falling = jnp.exp(rates[:, :, None] * lags)
    product = jnp.einsum("rci,rcj->cij", rising, falling, precision=lax.Precision.HIGH)
    lower = (lags[:, None] >= lags[None, :])[None]
    matrix = jnp.where(lower, product, 0.0)
    matrix = matrix + jnp.where(
        lags[:, None] == lags[None, :], skip_gain[:, None, None], 0.0
    )
    within = jnp.einsum(
        "cij,cbj->cbi", matrix.astype(jnp.bfloat16), blocks_in, preferred_element_type=jnp.float32
    )
    ending = jnp.exp(-rates[:, :, None] * (size - 1.0 - lags)).astype(jnp.bfloat16)
    ends = jnp.einsum("rcj,cbj->rbc", ending, blocks_in, preferred_element_type=jnp.float32)
    index = jnp.arange(count, dtype=jnp.float32)
    apart = index[:, None] - 1.0 - index[None, :]
    decay = jnp.where(
        (apart >= 0.0)[None, :, :, None],
        jnp.exp(-rates[:, None, None, :] * size * jnp.maximum(apart, 0.0)[None, :, :, None]),
        0.0,
    )
    entering = jnp.sum(decay * ends[:, None], axis=2)
    rise_decay = residues[:, :, None] * jnp.exp(-rates[:, :, None] * (lags + 1.0))
    before = jnp.einsum(
        "rci,rbc->cbi",
        rise_decay.astype(jnp.bfloat16),
        entering.astype(jnp.bfloat16),
        preferred_element_type=jnp.float32,
    )
    return (within + before).reshape(chan_count, seq_length)


def lagged_time(rows, weights):
    length = rows.shape[1]
    padded = jnp.concatenate([jnp.zeros_like(rows[:, :2]), rows], axis=1).astype(jnp.float32)
    running = weights[0][:, None] * padded[:, 2:]
    for lag_index in (1, 2):
        running = running + weights[lag_index][:, None] * padded[:, 2 - lag_index : 2 - lag_index + length]
    return running


def local(
    stream_in,
    mr_proj,
    mr_short,
    mr_filter,
    mr_out,
    li_gain,
    li_in,
    li_short,
    li_res,
    li_rate,
    li_skip,
):
    row_count = mr_proj.shape[0]
    chan_width = mr_proj.shape[2]
    tap_count = mr_filter.shape[1]
    filter_count = mr_filter.shape[0]
    seq_size = lax.axis_size("seq")
    chan_size = lax.axis_size("chan")
    width = stream_in.shape[1]
    own_count = chan_width // seq_size
    part = row_count // chan_size
    me = lax.axis_index("chan")

    out_weights = gathered_rows(1, mr_out)[0]
    out_weights, li_in, mr_proj = lax.optimization_barrier((out_weights, li_in, mr_proj))

    in_blocks = jnp.transpose(
        li_in.reshape(li_in.shape[0], 3, seq_size, own_count), (2, 1, 0, 3)
    )
    pieces = scattered(in_blocks, "seq")

    rim_rows = passed_along(mr_proj[-2:], "seq", 1)
    mr_mixed = lagged_rows(
        jnp.concatenate([rim_rows, mr_proj], axis=0).astype(jnp.float32), mr_short, row_count
    )
    queries = mr_mixed[:, 0]
    own_values = (mr_mixed[:, 1] * mr_mixed[:, 2]).astype(jnp.bfloat16)
    tail_rows = passed_along(own_values[-(tap_count - 1) :], "seq", 1)
    block_count = row_count // tap_count
    padded = jnp.concatenate(
        [tail_rows, own_values, jnp.zeros((1, chan_width), jnp.bfloat16)], axis=0
    )
    columns_major = padded.T.reshape(filter_count, GROUP, block_count + 1, tap_count)
    band_matrix = band_matrices(mr_filter)
    filtered_mr = jnp.einsum(
        "gis,gcbs->gcbi",
        band_matrix[:, :, :tap_count],
        columns_major[:, :, :-1],
        preferred_element_type=jnp.float32,
    )
    filtered_mr = filtered_mr + jnp.einsum(
        "gis,gcbs->gcbi",
        band_matrix[:, :, tap_count:],
        columns_major[:, :, 1:],
        preferred_element_type=jnp.float32,
    )
    filtered_rows = filtered_mr.reshape(chan_width, row_count).T
    gated = (queries * filtered_rows).astype(jnp.bfloat16)
    branch = branch_product(gated, out_weights)
    branch, pieces = lax.optimization_barrier((branch, pieces))
    in_own = assembled(pieces, "seq").reshape(width, 3 * own_count)
    summed = summed_rows(branch.reshape(chan_size, part, width), "chan")
    own_stream = lax.dynamic_slice_in_dim(stream_in, me * part, part, 0)
    stream = (own_stream.astype(jnp.float32) + summed).astype(jnp.bfloat16)
    stream_wide = stream.astype(jnp.float32)
    inverse_rms = lax.rsqrt(jnp.mean(stream_wide * stream_wide, axis=1, keepdims=True) + EPSILON)
    normed = (stream_wide * inverse_rms * li_gain[None]).astype(jnp.bfloat16)
    stream_parts = jnp.moveaxis(stream.reshape(part, chan_size, chan_width), 1, 0)
    if chan_size == 2:
        swap = [(0, 1), (1, 0)]
        stream_mine = lax.dynamic_index_in_dim(stream_parts, me, 0, keepdims=False)
        stream_other = lax.dynamic_index_in_dim(stream_parts, 1 - me, 0, keepdims=False)
        gathered, in_other, stream_other = gathered_rows(
            0, normed, in_own, stream_other
        )
        gathered = gathered.reshape(seq_size * part, width)
        stream_out = jnp.concatenate(
            [
                jnp.where(me == 0, stream_mine, stream_other),
                jnp.where(me == 0, stream_other, stream_mine),
            ]
        )

        def product(rows, matrix, low, high):
            return jnp.dot(
                rows,
                matrix[:, low * own_count : high * own_count],
                preferred_element_type=jnp.float32,
            ).astype(jnp.bfloat16)

        outgoing = product(gathered, in_other, 1, 3)
        sent = lax.ppermute(outgoing, "chan", swap)
        later, _ = lax.optimization_barrier((gathered, outgoing))
        outgoing_opener = product(later, in_other, 0, 1)
        sent_opener = lax.ppermute(outgoing_opener, "chan", swap)
        last, _ = lax.optimization_barrier((gathered, outgoing_opener))
        kept = product(last, in_own, 0, 3)
        received = (sent_opener, sent[:, :own_count], sent[:, own_count:])

        def ordered(index):
            mine = kept[:, index * own_count : (index + 1) * own_count].T
            theirs = received[index].T
            pair = [
                jnp.where(me == 0, mine, theirs).reshape(own_count, seq_size, 1, part),
                jnp.where(me == 0, theirs, mine).reshape(own_count, seq_size, 1, part),
            ]
            return jnp.concatenate(pair, axis=2).reshape(own_count, seq_size * row_count)
    else:
        stream_out = swapped(stream_parts, "chan").reshape(row_count, chan_width)
        gathered = gathered_rows(0, normed)[0].reshape(seq_size * part, width)
        in_all = lax.all_gather(in_own, "chan", axis=0)
        raw = jnp.einsum(
            "xdn,td->xnt", in_all, gathered, preferred_element_type=jnp.float32
        ).astype(jnp.bfloat16)
        raw = swapped(raw, "chan").reshape(chan_size, 3, own_count, seq_size, part)
        raw = jnp.transpose(raw, (1, 2, 3, 0, 4)).reshape(3, own_count, seq_size * row_count)

        def ordered(index):
            return raw[index]

    keys, gates = ordered(1), ordered(2)
    seq_offset = lax.axis_index("seq") * own_count
    own_short = lax.dynamic_slice_in_dim(li_short, seq_offset, own_count, 2)
    own_res = lax.dynamic_slice_in_dim(li_res, seq_offset, own_count, 1)
    own_rate = lax.dynamic_slice_in_dim(li_rate, seq_offset, own_count, 1)
    own_skip = lax.dynamic_slice_in_dim(li_skip, seq_offset, own_count, 0)
    values = (lagged_time(keys, own_short[1]) * lagged_time(gates, own_short[2])).astype(
        jnp.bfloat16
    )
    filtered = modal_filter(values, own_res, own_rate, own_skip)
    if chan_size == 2:
        filtered, sent_opener = lax.optimization_barrier((filtered, sent_opener))
        received = (sent_opener,) + received[1:]
    openers = ordered(0)
    result = (lagged_time(openers, own_short[0]) * filtered).astype(jnp.bfloat16)
    li_output = lax.all_to_all(result, "seq", split_axis=1, concat_axis=0, tiled=True)
    return (stream_out, li_output)


def solution(mesh):
    in_specs = (
        P("seq", None),
        P("seq", None, "chan"),
        P(None, None, "chan"),
        P("chan", None),
        P("chan", "seq"),
        P(),
        P("seq", None, "chan"),
        P(None, None, "chan"),
        P(None, "chan"),
        P(None, "chan"),
        P("chan"),
    )
    out_specs = (P("seq", "chan"), P("chan", "seq"))
    return jax.shard_map(local, mesh=mesh, in_specs=in_specs, out_specs=out_specs, check_vma=False)
```

```python
import functools

import jax
import jax.numpy as jnp
from jax import lax
from jax.experimental import pallas as pl
from jax.experimental.pallas import tpu as pltpu
from jax.sharding import PartitionSpec as P

GROUP = 16


EPSILON = 1e-06
HIGHEST = lax.Precision.HIGHEST


def passed_along(block, axis, distance):
    devices = range(lax.axis_size(axis))
    route = [(i - distance, i) for i in devices if i - distance in devices]
    return lax.ppermute(block, axis, route)


def band_matrices(filters):
    tap_count = filters.shape[1]
    out_index = jnp.arange(tap_count, dtype=jnp.int32)[:, None, None]
    in_index = jnp.arange(2 * tap_count, dtype=jnp.int32)[None, :, None]
    lag_index = jnp.arange(tap_count, dtype=jnp.int32)[None, None, :]
    selector = (out_index + tap_count - 1 - in_index == lag_index).astype(jnp.bfloat16)
    return jnp.einsum(
        "gj,isj->gis", filters.astype(jnp.bfloat16), selector, preferred_element_type=jnp.float32
    ).astype(jnp.bfloat16)


def lagged_rows(extended, weights, row_count):
    running = weights[:, 0][None] * extended[2 : 2 + row_count]
    for lag_index in (1, 2):
        running = (
            running
            + weights[:, lag_index][None] * extended[2 - lag_index : 2 - lag_index + row_count]
        )
    return running


def swapped(blocks, axis):
    count = lax.axis_size(axis)
    if count != 2:
        return lax.all_to_all(blocks, axis, split_axis=0, concat_axis=0, tiled=True)
    me = lax.axis_index(axis)
    mine = lax.dynamic_index_in_dim(blocks, me, 0, keepdims=False)
    other = lax.dynamic_index_in_dim(blocks, 1 - me, 0, keepdims=False)
    received = lax.ppermute(other, axis, [(0, 1), (1, 0)])
    first = me == 0
    return jnp.stack([jnp.where(first, mine, received), jnp.where(first, received, mine)])


def scattered(blocks, axis):
    count = lax.axis_size(axis)
    me = lax.axis_index(axis)
    chips, chip = count // 2, me // 2
    pairs = blocks.reshape((chips, 2) + blocks.shape[1:])
    pieces = []
    for k in range(chips):
        piece = lax.dynamic_index_in_dim(pairs, lax.rem(chip + k, chips), 0, keepdims=False)
        if k:
            route = [(i, (i + 2 * k) % count) for i in range(count)]
            piece = lax.ppermute(piece, axis, route)
        pieces.append(piece)
    return pieces


def assembled(pieces, axis):
    count = lax.axis_size(axis)
    me = lax.axis_index(axis)
    chips, chip, core = count // 2, me // 2, lax.rem(me, 2)
    kept = jnp.stack([lax.dynamic_index_in_dim(p, core, 0, keepdims=False) for p in pieces])
    given = jnp.stack([lax.dynamic_index_in_dim(p, 1 - core, 0, keepdims=False) for p in pieces])
    taken = lax.ppermute(given, axis, [(i, i ^ 1) for i in range(count)])
    both = jnp.stack(
        [jnp.where(core == 0, kept, taken), jnp.where(core == 0, taken, kept)], axis=1
    )
    both = both[::-1]
    return lax.dynamic_slice_in_dim(
        jnp.concatenate([both, both]), lax.rem(2 * chips - 1 - chip, chips), chips, 0
    )


def branch_kernel(gated_ref, weights_ref, out_ref):
    out_ref[...] = jnp.dot(gated_ref[...], weights_ref[0], preferred_element_type=jnp.float32)


def branch_product(gated, weights):
    rows, depth = gated.shape
    blocks, _, columns = weights.shape
    return pl.pallas_call(
        branch_kernel,
        out_shape=jax.ShapeDtypeStruct((rows, blocks * columns), jnp.float32),
        grid=(blocks,),
        in_specs=[
            pl.BlockSpec((rows, depth), lambda i: (0, 0)),
            pl.BlockSpec((1, depth, columns), lambda i: (i, 0, 0)),
        ],
        out_specs=pl.BlockSpec((rows, columns), lambda i: (0, i)),
        cost_estimate=pl.CostEstimate(
            flops=2 * rows * depth * blocks * columns,
            bytes_accessed=2 * blocks * depth * columns,
            transcendentals=0,
        ),
    )(gated, weights)


PARTS = 4


def ring_kernel(chips, swaps, *refs):
    inputs, outputs, sems = refs[: 1 + swaps], refs[1 + swaps : 2 + 2 * swaps], refs[2 + 2 * swaps :]
    block_ref, out_ref = inputs[0], outputs[0]
    ring_send, ring_recv, core_send, core_recv, own_sem, swap_send, swap_recv = sems
    me = lax.axis_index("seq")
    core = lax.rem(me, 2)
    chip = me // 2
    row, column = chip // 2, lax.rem(chip, 2)
    place = row + column * (chips - 1 - 2 * row)
    sibling = me + 1 - 2 * core
    rows = block_ref.shape[0] // PARTS

    def device(position, core_index):
        position = lax.rem(position + 2 * chips, chips)
        second = position // (chips // 2)
        at_row = position + second * (chips - 1 - 2 * position)
        return (2 * at_row + second) * 2 + core_index

    following, preceding = device(place + 1, core), device(place - 1, core)
    barrier = pltpu.get_barrier_semaphore()
    for target in (following, preceding, sibling):
        pl.semaphore_signal(barrier, inc=1, device_id={"seq": target})
    if swaps:
        partner = 1 - lax.axis_index("chan")
        pl.semaphore_signal(barrier, inc=1, device_id={"chan": partner})
    pl.semaphore_wait(barrier, 4 if swaps else 3)

    def ring(way, step, half, source, slot):
        part = pl.ds((2 * way + half) * rows, rows)
        index = (way * (chips - 1) + step) * 2 + half
        return pltpu.make_async_remote_copy(
            src_ref=source.at[part],
            dst_ref=out_ref.at[slot, part],
            send_sem=ring_send.at[index],
            recv_sem=ring_recv.at[index],
            device_id={"seq": (following, preceding)[way]},
        )

    def across(way, step, half, source, slot):
        part = pl.ds((2 * way + half) * rows, rows)
        index = (way * chips + step) * 2 + half
        return pltpu.make_async_remote_copy(
            src_ref=source.at[part],
            dst_ref=out_ref.at[slot, part],
            send_sem=core_send.at[index],
            recv_sem=core_recv.at[index],
            device_id={"seq": sibling},
        )

    started = []
    for step in range(chips):
        for half in (0, 1):
            for way in (0, 1):
                slot = device(place + (2 * way - 1) * step, core)
                source = block_ref if step == 0 else out_ref.at[slot]
                if step:
                    ring(way, step - 1, half, source, slot).wait_recv()
                if step < chips - 1:
                    copy = ring(way, step, half, source, slot)
                    copy.start()
                    started.append(copy)
                copy = across(way, step, half, source, slot)
                copy.start()
                started.append(copy)
        if step == 0:
            for i in range(swaps):
                copy = pltpu.make_async_remote_copy(
                    src_ref=inputs[1 + i],
                    dst_ref=outputs[1 + i],
                    send_sem=swap_send.at[i],
                    recv_sem=swap_recv.at[i],
                    device_id={"chan": partner},
                )
                copy.start()
                started.append(copy)
            own = pltpu.make_async_copy(block_ref, out_ref.at[me], own_sem)
            own.start()
    for step in range(chips):
        for half in (0, 1):
            for way in (0, 1):
                slot = device(place + (2 * way - 1) * step, 1 - core)
                across(way, step, half, out_ref.at[slot], slot).wait_recv()
    own.wait()
    for copy in started:
        copy.wait_send()
    for i in range(swaps):
        pltpu.make_async_remote_copy(
            src_ref=inputs[1 + i],
            dst_ref=outputs[1 + i],
            send_sem=swap_send.at[i],
            recv_sem=swap_recv.at[i],
            device_id={"chan": partner},
        ).wait_recv()


def gathered_rows(identity, block, *swapped_arrays):
    seq_size = lax.axis_size("seq")
    chips = seq_size // 2
    swaps = len(swapped_arrays)
    dma = pltpu.SemaphoreType.DMA
    results = pl.pallas_call(
        functools.partial(ring_kernel, chips, swaps),
        out_shape=[jax.ShapeDtypeStruct((seq_size,) + block.shape, block.dtype)]
        + [jax.ShapeDtypeStruct(a.shape, a.dtype) for a in swapped_arrays],
        in_specs=[pl.BlockSpec(memory_space=pl.ANY)] * (1 + swaps),
        out_specs=[pl.BlockSpec(memory_space=pl.ANY)] * (1 + swaps),
        scratch_shapes=[
            dma((4 * (chips - 1),)),
            dma((4 * (chips - 1),)),
            dma((4 * chips,)),
            dma((4 * chips,)),
            dma,
            dma((max(swaps, 1),)),
            dma((max(swaps, 1),)),
        ],
        compiler_params=pltpu.CompilerParams(collective_id=identity, has_side_effects=True),
    )(block, *swapped_arrays)
    return results


def summed_rows(blocks, axis):
    count = lax.axis_size(axis)
    if count != 2:
        return lax.psum_scatter(blocks.astype(jnp.bfloat16), axis, scatter_dimension=0).astype(
            jnp.float32
        )
    me = lax.axis_index(axis)
    mine = lax.dynamic_index_in_dim(blocks, me, 0, keepdims=False)
    other = lax.dynamic_index_in_dim(blocks, 1 - me, 0, keepdims=False).astype(jnp.bfloat16)
    return mine + lax.ppermute(other, axis, [(0, 1), (1, 0)]).astype(jnp.float32)


def modal_filter(values, residues, rates, skip_gain):
    chan_count, seq_length = values.shape
    size = min(128, seq_length)
    count = seq_length // size
    blocks_in = values.reshape(chan_count, count, size)
    lags = jnp.arange(size, dtype=jnp.float32)
    rising = residues[:, :, None] * jnp.exp(-rates[:, :, None] * lags)
    falling = jnp.exp(rates[:, :, None] * lags)
    product = jnp.einsum("rci,rcj->cij", rising, falling, precision=lax.Precision.HIGH)
    lower = (lags[:, None] >= lags[None, :])[None]
    matrix = jnp.where(lower, product, 0.0)
    matrix = matrix + jnp.where(
        lags[:, None] == lags[None, :], skip_gain[:, None, None], 0.0
    )
    within = jnp.einsum(
        "cij,cbj->cbi", matrix.astype(jnp.bfloat16), blocks_in, preferred_element_type=jnp.float32
    )
    ending = jnp.exp(-rates[:, :, None] * (size - 1.0 - lags)).astype(jnp.bfloat16)
    ends = jnp.einsum("rcj,cbj->rbc", ending, blocks_in, preferred_element_type=jnp.float32)
    index = jnp.arange(count, dtype=jnp.float32)
    apart = index[:, None] - 1.0 - index[None, :]
    decay = jnp.where(
        (apart >= 0.0)[None, :, :, None],
        jnp.exp(-rates[:, None, None, :] * size * jnp.maximum(apart, 0.0)[None, :, :, None]),
        0.0,
    )
    entering = jnp.sum(decay * ends[:, None], axis=2)
    rise_decay = residues[:, :, None] * jnp.exp(-rates[:, :, None] * (lags + 1.0))
    before = jnp.einsum(
        "rci,rbc->cbi",
        rise_decay.astype(jnp.bfloat16),
        entering.astype(jnp.bfloat16),
        preferred_element_type=jnp.float32,
    )
    return (within + before).reshape(chan_count, seq_length)


def lagged_time(rows, weights):
    length = rows.shape[1]
    padded = jnp.concatenate([jnp.zeros_like(rows[:, :2]), rows], axis=1).astype(jnp.float32)
    running = weights[0][:, None] * padded[:, 2:]
    for lag_index in (1, 2):
        running = running + weights[lag_index][:, None] * padded[:, 2 - lag_index : 2 - lag_index + length]
    return running


def local(
    stream_in,
    mr_proj,
    mr_short,
    mr_filter,
    mr_out,
    li_gain,
    li_in,
    li_short,
    li_res,
    li_rate,
    li_skip,
):
    row_count = mr_proj.shape[0]
    chan_width = mr_proj.shape[2]
    tap_count = mr_filter.shape[1]
    filter_count = mr_filter.shape[0]
    seq_size = lax.axis_size("seq")
    chan_size = lax.axis_size("chan")
    width = stream_in.shape[1]
    own_count = chan_width // seq_size
    part = row_count // chan_size
    me = lax.axis_index("chan")

    out_weights = gathered_rows(1, mr_out)[0]
    out_weights, li_in, mr_proj = lax.optimization_barrier((out_weights, li_in, mr_proj))

    in_blocks = jnp.transpose(
        li_in.reshape(li_in.shape[0], 3, seq_size, own_count), (2, 0, 1, 3)
    ).reshape(seq_size, li_in.shape[0], 3 * own_count)
    pieces = scattered(in_blocks, "seq")

    rim_rows = passed_along(mr_proj[-2:], "seq", 1)
    mr_mixed = lagged_rows(
        jnp.concatenate([rim_rows, mr_proj], axis=0).astype(jnp.float32), mr_short, row_count
    )
    queries = mr_mixed[:, 0]
    own_values = (mr_mixed[:, 1] * mr_mixed[:, 2]).astype(jnp.bfloat16)
    tail_rows = passed_along(own_values[-(tap_count - 1) :], "seq", 1)
    block_count = row_count // tap_count
    padded = jnp.concatenate(
        [tail_rows, own_values, jnp.zeros((1, chan_width), jnp.bfloat16)], axis=0
    )
    columns_major = padded.T.reshape(filter_count, GROUP, block_count + 1, tap_count)
    band_matrix = band_matrices(mr_filter)
    filtered_mr = jnp.einsum(
        "gis,gcbs->gcbi",
        band_matrix[:, :, :tap_count],
        columns_major[:, :, :-1],
        preferred_element_type=jnp.float32,
    )
    filtered_mr = filtered_mr + jnp.einsum(
        "gis,gcbs->gcbi",
        band_matrix[:, :, tap_count:],
        columns_major[:, :, 1:],
        preferred_element_type=jnp.float32,
    )
    filtered_rows = filtered_mr.reshape(chan_width, row_count).T
    gated = (queries * filtered_rows).astype(jnp.bfloat16)
    branch = branch_product(gated, out_weights)
    branch, pieces = lax.optimization_barrier((branch, pieces))
    in_own = assembled(pieces, "seq").reshape(width, 3 * own_count)
    summed = summed_rows(branch.reshape(chan_size, part, width), "chan")
    own_stream = lax.dynamic_slice_in_dim(stream_in, me * part, part, 0)
    stream = (own_stream.astype(jnp.float32) + summed).astype(jnp.bfloat16)
    stream_wide = stream.astype(jnp.float32)
    inverse_rms = lax.rsqrt(jnp.mean(stream_wide * stream_wide, axis=1, keepdims=True) + EPSILON)
    normed = (stream_wide * inverse_rms * li_gain[None]).astype(jnp.bfloat16)
    stream_parts = jnp.moveaxis(stream.reshape(part, chan_size, chan_width), 1, 0)
    if chan_size == 2:
        swap = [(0, 1), (1, 0)]
        stream_mine = lax.dynamic_index_in_dim(stream_parts, me, 0, keepdims=False)
        stream_other = lax.dynamic_index_in_dim(stream_parts, 1 - me, 0, keepdims=False)
        gathered, in_other, stream_other = gathered_rows(
            0, normed, in_own, stream_other
        )
        gathered = gathered.reshape(seq_size * part, width)
        stream_out = jnp.concatenate(
            [
                jnp.where(me == 0, stream_mine, stream_other),
                jnp.where(me == 0, stream_other, stream_mine),
            ]
        )

        def product(rows, matrix, low, high):
            return jnp.dot(
                rows,
                matrix[:, low * own_count : high * own_count],
                preferred_element_type=jnp.float32,
            ).astype(jnp.bfloat16)

        outgoing = product(gathered, in_other, 1, 3)
        sent = lax.ppermute(outgoing, "chan", swap)
        later, _ = lax.optimization_barrier((gathered, outgoing))
        outgoing_opener = product(later, in_other, 0, 1)
        sent_opener = lax.ppermute(outgoing_opener, "chan", swap)
        last, _ = lax.optimization_barrier((gathered, outgoing_opener))
        kept = product(last, in_own, 0, 3)
        kept, li_rate = lax.optimization_barrier((kept, li_rate))
        received = (sent_opener, sent[:, :own_count], sent[:, own_count:])

        def ordered(index):
            mine = kept[:, index * own_count : (index + 1) * own_count].T
            theirs = received[index].T
            pair = [
                jnp.where(me == 0, mine, theirs).reshape(own_count, seq_size, 1, part),
                jnp.where(me == 0, theirs, mine).reshape(own_count, seq_size, 1, part),
            ]
            return jnp.concatenate(pair, axis=2).reshape(own_count, seq_size * row_count)
    else:
        stream_out = swapped(stream_parts, "chan").reshape(row_count, chan_width)
        gathered = gathered_rows(0, normed)[0].reshape(seq_size * part, width)
        in_all = lax.all_gather(in_own, "chan", axis=0)
        raw = jnp.einsum(
            "xdn,td->xnt", in_all, gathered, preferred_element_type=jnp.float32
        ).astype(jnp.bfloat16)
        raw = swapped(raw, "chan").reshape(chan_size, 3, own_count, seq_size, part)
        raw = jnp.transpose(raw, (1, 2, 3, 0, 4)).reshape(3, own_count, seq_size * row_count)

        def ordered(index):
            return raw[index]

    keys, gates = ordered(1), ordered(2)
    seq_offset = lax.axis_index("seq") * own_count
    own_short = lax.dynamic_slice_in_dim(li_short, seq_offset, own_count, 2)
    own_res = lax.dynamic_slice_in_dim(li_res, seq_offset, own_count, 1)
    own_rate = lax.dynamic_slice_in_dim(li_rate, seq_offset, own_count, 1)
    own_skip = lax.dynamic_slice_in_dim(li_skip, seq_offset, own_count, 0)
    values = (lagged_time(keys, own_short[1]) * lagged_time(gates, own_short[2])).astype(
        jnp.bfloat16
    )
    filtered = modal_filter(values, own_res, own_rate, own_skip)
    if chan_size == 2:
        filtered, sent_opener = lax.optimization_barrier((filtered, sent_opener))
        received = (sent_opener,) + received[1:]
    openers = ordered(0)
    result = (lagged_time(openers, own_short[0]) * filtered).astype(jnp.bfloat16)
    li_output = lax.all_to_all(result, "seq", split_axis=1, concat_axis=0, tiled=True)
    return (stream_out, li_output)


def solution(mesh):
    in_specs = (
        P("seq", None),
        P("seq", None, "chan"),
        P(None, None, "chan"),
        P("chan", None),
        P("chan", "seq"),
        P(),
        P("seq", None, "chan"),
        P(None, None, "chan"),
        P(None, "chan"),
        P(None, "chan"),
        P("chan"),
    )
    out_specs = (P("seq", "chan"), P("chan", "seq"))
    return jax.shard_map(local, mesh=mesh, in_specs=in_specs, out_specs=out_specs, check_vma=False)
```
